256 devices in a mesh: head: 4 (over x_hi, core), vis: 32 (over y, z), sec: 2 (over x_lo).
Axes of the slice: x: 4 (x_hi: 2, x_lo: 2; x = x_hi * 2 + x_lo), y: 4, z: 8, core: 2. Of those that a mesh axis runs over, the one named last changes fastest.
Arguments:
- text_states: bfloat16 [256, 8192], P(None, 'vis'), may hold values from -6 to 6
- w_query: bfloat16 [8192, 8192], P('vis', ('head', 'sec')), may hold values from -0.0625 to 0.0625
- w_out: bfloat16 [8192, 8192], P(('head', 'sec'), 'vis'), may hold values from -0.25 to 0.25
- visual_keys: bfloat16 [262144, 1024], P('vis', ('head', 'sec')), may hold values from -120 to 120
- visual_values: bfloat16 [262144, 1024], P('vis', ('head', 'sec')), may hold values from -6 to 6
- block_list: int32 [2, 32, 32], P(None, 'vis'), may hold values from -1 to 63, as said below
Outputs:
- projected: bfloat16 [256, 8192], P(('head', 'sec'), 'vis')
The draws below stay inside these ranges and needn't reach their ends.
Inputs may be any that keep to these rules, and one draw needn't show every extreme that they name: `block_list`: for each query block and shard, the entries that are not -1 are distinct and come first; each query block selects exactly 512 key blocks in all (a quarter), between 0 and 32 from one shard, and exactly 32 from some shard.
All inputs are finite; a program needn't handle non-finite values.
Results may differ from the reference program's by a relative error of at most 0.012.
Values may be sent and summed in bfloat16 or wider, within the bound.
No kernel may reach another device: no remote copies, remote signals or barrier semaphores. Data moves between devices by JAX's collectives and lax.ppermute only.
A program may use at most 192 MiB of HBM per device.

```python
import jax
import jax.numpy as jnp
from jax import lax

D = 8192
QUERY_HEADS = 64
KEY_VALUE_HEADS = 8
HEAD_SIZE = 128
BLOCK_TOKENS = 128
TOK = 256
SHARDS = 32
VISUAL_TOKENS = 262144
BLK_DEV = 64
MEANB = 16
MAXB = 32
QUERY_BLOCK_COUNT = 2


def draw_block_list(key, part):
    key_pair, key_shift, key_pick = jax.random.split(jax.random.fold_in(key, 11), 3)
    row_keys = jax.random.split(key_pair, QUERY_BLOCK_COUNT)

    def shard_order(sub_key):
        return jax.random.permutation(sub_key, SHARDS)
    order = jax.vmap(shard_order)(row_keys)
    shift = jax.random.randint(key_shift, (QUERY_BLOCK_COUNT, SHARDS // 2), 0, MEANB + 1)
    shift = shift.at[:, 0].set(MEANB)
    row_index = jnp.arange(QUERY_BLOCK_COUNT)[:, None]
    counts = jnp.zeros((QUERY_BLOCK_COUNT, SHARDS), jnp.int32)
    counts = counts.at[row_index, order[:, 0::2]].set(MEANB + shift)
    counts = counts.at[row_index, order[:, 1::2]].set(MEANB - shift)
    pick_keys = jax.random.split(key_pick, QUERY_BLOCK_COUNT * SHARDS)

    def block_order(sub_key):
        return jax.random.permutation(sub_key, BLK_DEV)[:MAXB]
    picks = jax.vmap(block_order)(pick_keys).reshape(QUERY_BLOCK_COUNT, SHARDS, MAXB)
    slot_index = jnp.arange(MAXB)[None, None, :]
    return jnp.where(slot_index < counts[:, :, None], picks, -1).astype(jnp.int32)


def draw_visual_keys(key, part):
    base_key = jax.random.fold_in(jax.random.fold_in(key, 23), 0)
    key_column_width = KEY_VALUE_HEADS * HEAD_SIZE
    drawn = 1.25 * jnp.clip(jax.random.normal(base_key, (VISUAL_TOKENS, key_column_width), jnp.float32), -6.0, 6.0)
    return drawn.astype(jnp.bfloat16)


def level_of(rng, dims, cuts, smallest, largest):
    level, own = 1.0, jax.random.fold_in(rng, 6)
    for position, parts in cuts:
        draws = jnp.exp(jax.random.uniform(jax.random.fold_in(own, position), (parts,), jnp.float32, smallest / len(cuts), largest / len(cuts)))
        level = level * jnp.repeat(draws, dims[position] // parts).reshape([-1 if axis == position else 1 for axis in range(len(dims))])
    return level


def gaussian(own_key, dims, spread, bound, pieces=(), kind=jnp.bfloat16):
    array = jax.random.normal(own_key, dims, jnp.float32) * spread
    if len(pieces) > 0:
        array = level_of(own_key, dims, pieces, -0.22, 0.18) * array
    return jnp.clip(array, min=-bound, max=bound).astype(kind)


def setup_inputs(seed: int = 0) -> dict:
    splits = jax.random.split(jax.random.key(seed), 7)
    text_states = gaussian(splits[0], (TOK, D), 1.0, 6.0, ((1, 32),))
    w_query = gaussian(splits[1], (D, QUERY_HEADS * HEAD_SIZE), D ** -0.5, 0.0625, ((0, 32), (1, 8)))
    w_out = gaussian(splits[2], (QUERY_HEADS * HEAD_SIZE, D), (QUERY_HEADS * HEAD_SIZE // 16) ** -0.5, 0.25, ((0, 8), (1, 32)))
    visual_keys = draw_visual_keys(jax.random.fold_in(splits[6], 71), 0)
    visual_values = gaussian(splits[4], (VISUAL_TOKENS, KEY_VALUE_HEADS * HEAD_SIZE), 1.0, 6.0, ((0, 32), (1, 8)))
    block_list = draw_block_list(jax.random.fold_in(splits[6], 71), 0)
    return dict(text_states=text_states, w_query=w_query, w_out=w_out, visual_keys=visual_keys, visual_values=visual_values, block_list=block_list)


def reference(text_states, w_query, w_out, visual_keys, visual_values, block_list):
    queries_per_group = QUERY_HEADS // KEY_VALUE_HEADS
    query_matrix = jnp.dot(text_states, w_query, preferred_element_type=jnp.float32).astype(jnp.bfloat16)
    blocked_queries = query_matrix.reshape(QUERY_BLOCK_COUNT, BLOCK_TOKENS, KEY_VALUE_HEADS, queries_per_group, HEAD_SIZE)
    blocked_keys = visual_keys.reshape(VISUAL_TOKENS // BLOCK_TOKENS, BLOCK_TOKENS, KEY_VALUE_HEADS, HEAD_SIZE)
    blocked_values = visual_values.reshape(VISUAL_TOKENS // BLOCK_TOKENS, BLOCK_TOKENS, KEY_VALUE_HEADS, HEAD_SIZE)
    offsets = (jnp.arange(SHARDS, dtype=jnp.int32) * BLK_DEV)[:, None]

    def one_block(packed):
        query_block, block_ids = packed
        present = (block_ids >= 0).reshape(-1)
        chosen = (jnp.maximum(block_ids, 0).astype(jnp.int32) + offsets).reshape(-1).astype(jnp.int32)
        key_rows = jnp.moveaxis(blocked_keys[chosen], 2, 0)
        value_rows = jnp.moveaxis(blocked_values[chosen], 2, 0)
        head_queries = jnp.moveaxis(query_block, 1, 0)

        def one_head(inner):
            query_head, key_head, value_head = inner
            scores = jnp.einsum("tqd,nbd->tqnb", query_head.astype(jnp.float32), key_head.astype(jnp.float32)) * (HEAD_SIZE ** -0.5)
            keep_mask = present[None, None, :, None]
            scores = jnp.where(keep_mask, scores, -1.0e30)
            top_score = jnp.max(scores, axis=(2, 3))
            raised = jnp.where(keep_mask, jnp.exp(scores - top_score[:, :, None, None]), 0.0)
            denom_sum = jnp.sum(raised, axis=(2, 3))
            weighted = jnp.einsum("tqnb,nbd->tqd", raised.astype(jnp.bfloat16).astype(jnp.float32), value_head.astype(jnp.float32))
            return weighted / denom_sum[:, :, None]

        result = lax.map(one_head, (head_queries, key_rows, value_rows))
        return jnp.moveaxis(result, 0, 1)

    attended = lax.map(one_block, (blocked_queries, block_list))
    attended = attended.reshape(TOK, QUERY_HEADS * HEAD_SIZE).astype(jnp.bfloat16)
    return jnp.dot(attended, w_out, preferred_element_type=jnp.float32).astype(jnp.bfloat16)
```

```python
import functools

import jax
import jax.numpy as jnp
import numpy as np
from jax import lax
from jax.experimental import pallas as pl
from jax.experimental.pallas import tpu as pltpu
from jax.sharding import Mesh, PartitionSpec as P

HEAD_SIZE = 128
BLOCK_TOKENS = 128
CHUNK = 4
NEG_FILL = -1e30
EXP2_SCALE = float(np.log2(np.e) / np.sqrt(HEAD_SIZE))


def split3(x):
    hi = x.astype(jnp.bfloat16).astype(jnp.float32)
    rest = x - hi
    mid = rest.astype(jnp.bfloat16).astype(jnp.float32)
    return hi, mid, rest - mid


def pack_stats(top, total, heads):
    lane = lax.broadcasted_iota(jnp.int32, top[0].shape, 1)
    packed = jnp.zeros(top[0].shape, jnp.float32)
    for h in range(heads):
        for i, piece in enumerate((*split3(top[h]), *split3(total[h]))):
            packed = jnp.where(lane == i * heads + h, piece, packed)
    return packed.astype(jnp.bfloat16)


def attention_kernel(heads, ids_ref, q_ref, k_ref, v_ref, out_ref, q_rows, top_ref, acc_ref):
    qb = q_ref.shape[0] // BLOCK_TOKENS
    slots = ids_ref.shape[1]
    rows = heads * BLOCK_TOKENS
    for b in range(qb):
        t0 = b * BLOCK_TOKENS
        for h in range(heads):
            q_rows[h * 128 : (h + 1) * 128, :] = q_ref[t0 : t0 + 128, h * 128 : (h + 1) * 128]
        top_ref[...] = jnp.full(top_ref.shape, NEG_FILL, jnp.float32)
        acc_ref[...] = jnp.zeros(acc_ref.shape, jnp.float32)
        count = lax.fori_loop(
            0, slots, lambda j, c: c + (ids_ref[b, j] >= 0).astype(jnp.int32), jnp.int32(0)
        )

        def chunk(c, carry):
            ks, vs = [], []
            for i in range(CHUNK):
                j = c * CHUNK + i
                block = ids_ref[b, jnp.minimum(j, count - 1)]
                start = pl.multiple_of(block * BLOCK_TOKENS, BLOCK_TOKENS)
                live = jnp.where(j < count, 1.0, 0.0).astype(jnp.float32)
                ks.append(k_ref[pl.ds(start, BLOCK_TOKENS), :])
                value = v_ref[pl.ds(start, BLOCK_TOKENS), :].astype(jnp.float32) * live
                flag = jnp.full((BLOCK_TOKENS, 128), 1.0, jnp.float32) * live
                vs.append(jnp.concatenate([value, flag], axis=1).astype(jnp.bfloat16))
            kc = jnp.concatenate(ks, axis=0)
            vc = jnp.concatenate(vs, axis=0)
            tile = 256
            for r in range(rows // tile):
                rs = pl.ds(r * tile, tile)
                s = lax.dot_general(
                    q_rows[rs, :], kc, (((1,), (1,)), ((), ())), preferred_element_type=jnp.float32
                )
                old = top_ref[rs, :]
                new = jnp.maximum(old, jnp.max(s, axis=1, keepdims=True))
                alpha = jnp.exp2((old - new) * EXP2_SCALE)
                wide = jnp.concatenate([new] * CHUNK, axis=1)
                p = jnp.exp2((s - wide) * EXP2_SCALE).astype(jnp.bfloat16)
                pv = jnp.dot(p, vc, preferred_element_type=jnp.float32)
                acc_ref[rs, :] = acc_ref[rs, :] * jnp.concatenate([alpha, alpha], axis=1) + pv
                top_ref[rs, :] = new
            return carry

        lax.fori_loop(0, (count + CHUNK - 1) // CHUNK, chunk, 0)
        tops, totals = [], []
        for h in range(heads):
            hr = slice(h * 128, (h + 1) * 128)
            out_ref[t0 : t0 + 128, hr] = acc_ref[hr, :128].astype(jnp.bfloat16)
            tops.append(top_ref[hr, :])
            totals.append(acc_ref[hr, 128:])
        out_ref[t0 : t0 + 128, heads * 128 :] = pack_stats(tops, totals, heads)


def attention(ids, q, k, v):
    heads = q.shape[1] // HEAD_SIZE
    rows = heads * BLOCK_TOKENS
    vmem = pl.BlockSpec(memory_space=pltpu.VMEM)
    return pl.pallas_call(
        functools.partial(attention_kernel, heads),
        out_shape=jax.ShapeDtypeStruct((q.shape[0], q.shape[1] + 128), jnp.bfloat16),
        in_specs=[pl.BlockSpec(memory_space=pltpu.SMEM), vmem, vmem, vmem],
        out_specs=vmem,
        scratch_shapes=[
            pltpu.VMEM((rows, 128), jnp.bfloat16),
            pltpu.VMEM((rows, 128), jnp.float32),
            pltpu.VMEM((rows, 256), jnp.float32),
        ],
        name="attend",
    )(ids, q, k, v)


def merge_kernel(heads, final, parts_ref, out_ref):
    sources, rows = parts_ref.shape[0], parts_ref.shape[1]
    wide = heads * 128
    step = 8
    for r in range(0, rows, step):
        rs = slice(r, r + step)

        def gather3(stats, first):
            total = stats if first == 0 else pltpu.roll(stats, 128 - first * heads, 1)
            for i in (1, 2):
                total = total + pltpu.roll(stats, 128 - (first + i) * heads, 1)
            return total

        stats = [parts_ref[s, rs, wide:].astype(jnp.float32) for s in range(sources)]
        tops = [gather3(x, 0) for x in stats]
        top = functools.reduce(jnp.maximum, tops)
        scales = [jnp.exp2((t - top) * EXP2_SCALE) for t in tops]
        total = functools.reduce(
            jnp.add, [gather3(x, 3) * scale for x, scale in zip(stats, scales)]
        )
        for h in range(heads):
            hc = slice(h * 128, (h + 1) * 128)
            acc = jnp.zeros((step, 128), jnp.float32)
            for s in range(sources):
                acc = acc + scales[s][:, h : h + 1] * parts_ref[s, rs, hc].astype(jnp.float32)
            if final:
                acc = acc / total[:, h : h + 1]
            out_ref[rs, hc] = acc.astype(jnp.bfloat16)
        if not final:
            spread = lambda x: [
                jnp.broadcast_to(x[:, h : h + 1], (step, 128)) for h in range(heads)
            ]
            out_ref[rs, wide:] = pack_stats(spread(top), spread(total), heads)


def merge(parts, final):
    width = parts.shape[2]
    heads = width // 128 - 1
    vmem = pl.BlockSpec(memory_space=pltpu.VMEM)
    return pl.pallas_call(
        functools.partial(merge_kernel, heads, final),
        out_shape=jax.ShapeDtypeStruct(
            (parts.shape[1], width - 128 if final else width), jnp.bfloat16
        ),
        in_specs=[vmem],
        out_specs=vmem,
        name="merge",
    )(parts)


def swap(x, axis):
    return lax.all_to_all(x, axis, 0, 0, tiled=True)


def gather(x, axis):
    size = lax.axis_size(axis)
    out = swap(jnp.broadcast_to(x[None], (size, *x.shape)), axis)
    return out.reshape(size * x.shape[0], *x.shape[1:])


def scatter_sum(x, axis):
    size = lax.axis_size(axis)
    parts = swap(x.reshape(size, x.shape[0] // size, *x.shape[1:]), axis)
    return functools.reduce(jnp.add, [parts[i].astype(jnp.float32) for i in range(size)])


def on_device(text_states, w_query, w_out, visual_keys, visual_values, block_list):
    terms = jnp.dot(text_states, w_query, preferred_element_type=jnp.float32)
    terms = scatter_sum(terms.astype(jnp.bfloat16), "y")
    terms = scatter_sum(terms.astype(jnp.bfloat16), "z")
    query = gather(gather(terms.astype(jnp.bfloat16), "z"), "y")
    ids = block_list[:, 0, :]
    partial = attention(ids, query, visual_keys, visual_values)
    ny, nz = lax.axis_size("y"), lax.axis_size("z")
    part = merge(swap(partial.reshape(ny, -1, partial.shape[1]), "y"), False)
    attended = merge(swap(part.reshape(nz, -1, part.shape[1]), "z"), True)
    attended = gather(gather(attended, "z"), "y")
    out = jnp.dot(attended, w_out, preferred_element_type=jnp.float32)
    return scatter_sum(out.astype(jnp.bfloat16), ("head", "sec")).astype(jnp.bfloat16)


def solution(mesh):
    heads, vis, sec = (mesh.shape[a] for a in ("head", "vis", "sec"))
    ny = 4 if vis % 4 == 0 and vis > 4 else 2
    fine = Mesh(mesh.devices.reshape(heads, ny, vis // ny, sec), ("head", "y", "z", "sec"))
    vy, hs = ("y", "z"), ("head", "sec")
    in_specs = (
        P(None, vy),
        P(vy, hs),
        P(hs, vy),
        P(vy, hs),
        P(vy, hs),
        P(None, vy, None),
    )
    return jax.shard_map(
        on_device, mesh=fine, in_specs=in_specs, out_specs=P(hs, vy), check_vma=False
    )
```

```python
import functools

import jax
import jax.numpy as jnp
import numpy as np
from jax import lax
from jax.experimental import pallas as pl
from jax.experimental.pallas import tpu as pltpu
from jax.sharding import Mesh, PartitionSpec as P

HEAD_SIZE = 128
BLOCK_TOKENS = 128
BIG, SMALL, TILE = 8, 4, 128
NEG_FILL = -1e30
EXP2_SCALE = float(np.log2(np.e) / np.sqrt(HEAD_SIZE))


def split3(x):
    hi = x.astype(jnp.bfloat16).astype(jnp.float32)
    rest = x - hi
    mid = rest.astype(jnp.bfloat16).astype(jnp.float32)
    return hi, mid, rest - mid


def pack_stats(top, total, heads):
    lane = lax.broadcasted_iota(jnp.int32, top[0].shape, 1)
    both = jnp.zeros(top[0].shape, jnp.float32)
    for h in range(heads):
        both = jnp.where(lane == h, top[h], both)
        both = jnp.where(lane == 3 * heads + h, total[h], both)
    hi, mid, low = split3(both)
    packed = hi + pltpu.roll(mid, heads, 1) + pltpu.roll(low, 2 * heads, 1)
    return packed.astype(jnp.bfloat16)


def attention_kernel(heads, ids_ref, q_ref, k_ref, v_ref, out_ref, q_rows, top_ref, acc_ref):
    query_blocks = q_ref.shape[0] // BLOCK_TOKENS
    slots = ids_ref.shape[1]
    rows = heads * BLOCK_TOKENS

    def query_block(b, carry):
        tokens = pl.ds(pl.multiple_of(b * BLOCK_TOKENS, BLOCK_TOKENS), BLOCK_TOKENS)
        for h in range(heads):
            hc = slice(h * 128, (h + 1) * 128)
            q_rows[hc, :] = q_ref[tokens, hc]
        top_ref[...] = jnp.full(top_ref.shape, NEG_FILL, jnp.float32)
        acc_ref[...] = jnp.zeros(acc_ref.shape, jnp.float32)
        count = lax.fori_loop(
            0, slots, lambda j, c: c + (ids_ref[b, j] >= 0).astype(jnp.int32), jnp.int32(0)
        )

        def blocks(first, size, masked):
            ks, vs = [], []
            for i in range(size):
                j = first + i
                block = ids_ref[b, jnp.minimum(j, count - 1) if masked else j]
                start = pl.multiple_of(block * BLOCK_TOKENS, BLOCK_TOKENS)
                ks.append(k_ref[pl.ds(start, BLOCK_TOKENS), :])
                value = v_ref[pl.ds(start, BLOCK_TOKENS), :]
                flag = jnp.full((BLOCK_TOKENS, 128), 1.0, jnp.bfloat16)
                if masked:
                    live = jnp.where(j < count, 1.0, 0.0).astype(jnp.float32)
                    value = (value.astype(jnp.float32) * live).astype(jnp.bfloat16)
                    flag = (jnp.full((BLOCK_TOKENS, 128), 1.0, jnp.float32) * live).astype(jnp.bfloat16)
                vs.append(jnp.concatenate([value, flag], axis=1))
            kc = jnp.concatenate(ks, axis=0)
            vc = jnp.concatenate(vs, axis=0)
            for r in range(rows // TILE):
                rs = pl.ds(r * TILE, TILE)
                s = lax.dot_general(
                    q_rows[rs, :], kc, (((1,), (1,)), ((), ())), preferred_element_type=jnp.float32
                )
                old = top_ref[rs, :]
                new = jnp.maximum(old, jnp.max(s, axis=1, keepdims=True))
                alpha = jnp.exp2((old - new) * EXP2_SCALE)
                wide = jnp.concatenate([new] * size, axis=1)
                p = jnp.exp2((s - wide) * EXP2_SCALE).astype(jnp.bfloat16)
                pv = jnp.dot(p, vc, preferred_element_type=jnp.float32)
                acc_ref[rs, :] = acc_ref[rs, :] * jnp.concatenate([alpha, alpha], axis=1) + pv
                top_ref[rs, :] = new

        full = count // BIG

        def big(c, carry):
            blocks(c * BIG, BIG, False)
            return carry

        def small(c, carry):
            blocks(full * BIG + c * SMALL, SMALL, True)
            return carry

        lax.fori_loop(0, full, big, 0)
        lax.fori_loop(0, (count - full * BIG + SMALL - 1) // SMALL, small, 0)
        tops, totals = [], []
        for h in range(heads):
            hc = slice(h * 128, (h + 1) * 128)
            out_ref[tokens, hc] = acc_ref[hc, :128].astype(jnp.bfloat16)
            tops.append(top_ref[hc, :])
            totals.append(acc_ref[hc, 128:])
        out_ref[tokens, heads * 128 :] = pack_stats(tops, totals, heads)
        return carry

    lax.fori_loop(0, query_blocks, query_block, 0)


def attention(ids, q, k, v):
    heads = q.shape[1] // HEAD_SIZE
    rows = heads * BLOCK_TOKENS
    vmem = pl.BlockSpec(memory_space=pltpu.VMEM)
    k = pltpu.with_memory_space_constraint(k, pltpu.VMEM)
    v = pltpu.with_memory_space_constraint(v, pltpu.VMEM)
    return pl.pallas_call(
        functools.partial(attention_kernel, heads),
        out_shape=jax.ShapeDtypeStruct((q.shape[0], q.shape[1] + 128), jnp.bfloat16),
        in_specs=[pl.BlockSpec(memory_space=pltpu.SMEM), vmem, vmem, vmem],
        out_specs=vmem,
        scratch_shapes=[
            pltpu.VMEM((rows, 128), jnp.bfloat16),
            pltpu.VMEM((rows, 128), jnp.float32),
            pltpu.VMEM((rows, 256), jnp.float32),
        ],
        compiler_params=pltpu.CompilerParams(vmem_limit_bytes=24 * 2**20),
        name="attend",
    )(ids, q, k, v)


def merge_kernel(heads, final, parts_ref, out_ref):
    sources, rows = parts_ref.shape[0], parts_ref.shape[1]
    wide = heads * 128
    step = 8
    for r in range(0, rows, step):
        rs = slice(r, r + step)

        def gather3(stats, first):
            total = stats if first == 0 else pltpu.roll(stats, 128 - first * heads, 1)
            for i in (1, 2):
                total = total + pltpu.roll(stats, 128 - (first + i) * heads, 1)
            return total

        stats = [parts_ref[s, rs, wide:].astype(jnp.float32) for s in range(sources)]
        tops = [gather3(x, 0) for x in stats]
        top = functools.reduce(jnp.maximum, tops)
        scales = [jnp.exp2((t - top) * EXP2_SCALE) for t in tops]
        total = functools.reduce(
            jnp.add, [gather3(x, 3) * scale for x, scale in zip(stats, scales)]
        )
        for h in range(heads):
            hc = slice(h * 128, (h + 1) * 128)
            acc = jnp.zeros((step, 128), jnp.float32)
            for s in range(sources):
                acc = acc + scales[s][:, h : h + 1] * parts_ref[s, rs, hc].astype(jnp.float32)
            if final:
                acc = acc / total[:, h : h + 1]
            out_ref[rs, hc] = acc.astype(jnp.bfloat16)
        if not final:
            spread = lambda x: [
                jnp.broadcast_to(x[:, h : h + 1], (step, 128)) for h in range(heads)
            ]
            out_ref[rs, wide:] = pack_stats(spread(top), spread(total), heads)


def merge(parts, final):
    width = parts.shape[2]
    heads = width // 128 - 1
    vmem = pl.BlockSpec(memory_space=pltpu.VMEM)
    return pl.pallas_call(
        functools.partial(merge_kernel, heads, final),
        out_shape=jax.ShapeDtypeStruct(
            (parts.shape[1], width - 128 if final else width), jnp.bfloat16
        ),
        in_specs=[vmem],
        out_specs=vmem,
        name="merge",
    )(parts)


def swap(x, axis):
    return lax.all_to_all(x, axis, 0, 0, tiled=True)


def gather(x, axis):
    size = lax.axis_size(axis)
    out = swap(jnp.broadcast_to(x[None], (size, *x.shape)), axis)
    return out.reshape(size * x.shape[0], *x.shape[1:])


def scatter_sum(x, axis):
    size = lax.axis_size(axis)
    parts = swap(x.reshape(size, x.shape[0] // size, *x.shape[1:]), axis)
    return functools.reduce(jnp.add, [parts[i].astype(jnp.float32) for i in range(size)])


def on_device(text_states, w_query, w_out, visual_keys, visual_values, block_list):
    vis = ("y", "z")
    shards = lax.axis_size(vis)
    terms = jnp.dot(text_states, w_query, preferred_element_type=jnp.float32)
    terms = scatter_sum(terms.astype(jnp.bfloat16), vis)
    query = gather(gather(terms.astype(jnp.bfloat16), "z"), "y")
    ids = block_list[:, 0, :]
    partial = attention(ids, query, visual_keys, visual_values)
    attended = merge(swap(partial.reshape(shards, -1, partial.shape[1]), vis), True)
    attended = gather(gather(attended, "z"), "y")
    out = jnp.dot(attended, w_out, preferred_element_type=jnp.float32)
    return scatter_sum(out.astype(jnp.bfloat16), ("head", "sec")).astype(jnp.bfloat16)


def solution(mesh):
    heads, vis, sec = (mesh.shape[a] for a in ("head", "vis", "sec"))
    ny = 4 if vis % 4 == 0 and vis > 4 else 2
    fine = Mesh(mesh.devices.reshape(heads, ny, vis // ny, sec), ("head", "y", "z", "sec"))
    vy, hs = ("y", "z"), ("head", "sec")
    in_specs = (
        P(None, vy),
        P(vy, hs),
        P(hs, vy),
        P(vy, hs),
        P(vy, hs),
        P(None, vy, None),
    )
    return jax.shard_map(
        on_device, mesh=fine, in_specs=in_specs, out_specs=P(hs, vy), check_vma=False
    )
```

```python
import functools

import jax
import jax.numpy as jnp
import numpy as np
from jax import lax
from jax.experimental import pallas as pl
from jax.experimental.pallas import tpu as pltpu
from jax.sharding import Mesh, PartitionSpec as P

HEAD_SIZE = 128
BLOCK_TOKENS = 128
BIG, SMALL, TILE = 8, 4, 128
NEG_FILL = -1e30
EXP2_SCALE = float(np.log2(np.e) / np.sqrt(HEAD_SIZE))


def split3(x):
    hi = x.astype(jnp.bfloat16).astype(jnp.float32)
    rest = x - hi
    mid = rest.astype(jnp.bfloat16).astype(jnp.float32)
    return hi, mid, rest - mid


def pack_stats(top, total, heads):
    lane = lax.broadcasted_iota(jnp.int32, top[0].shape, 1)
    both = jnp.zeros(top[0].shape, jnp.float32)
    for h in range(heads):
        both = jnp.where(lane == h, top[h], both)
        both = jnp.where(lane == 3 * heads + h, total[h], both)
    hi, mid, low = split3(both)
    packed = hi + pltpu.roll(mid, heads, 1) + pltpu.roll(low, 2 * heads, 1)
    return packed.astype(jnp.bfloat16)


def attention_kernel(heads, ids_ref, q_ref, k_ref, v_ref, out_ref, q_rows, top_ref, acc_ref):
    query_blocks = q_ref.shape[0] // BLOCK_TOKENS
    slots = ids_ref.shape[1]
    rows = heads * BLOCK_TOKENS

    def query_block(b, carry):
        tokens = pl.ds(pl.multiple_of(b * BLOCK_TOKENS, BLOCK_TOKENS), BLOCK_TOKENS)
        for h in range(heads):
            hc = slice(h * 128, (h + 1) * 128)
            q_rows[hc, :] = q_ref[tokens, hc]
        top_ref[...] = jnp.full(top_ref.shape, NEG_FILL, jnp.float32)
        acc_ref[...] = jnp.zeros(acc_ref.shape, jnp.float32)
        count = lax.fori_loop(
            0, slots, lambda j, c: c + (ids_ref[b, j] >= 0).astype(jnp.int32), jnp.int32(0)
        )

        def blocks(first, size, masked):
            ks, vs = [], []
            for i in range(size):
                j = first + i
                block = ids_ref[b, jnp.minimum(j, count - 1) if masked else j]
                start = pl.multiple_of(block * BLOCK_TOKENS, BLOCK_TOKENS)
                ks.append(k_ref[pl.ds(start, BLOCK_TOKENS), :])
                value = v_ref[pl.ds(start, BLOCK_TOKENS), :]
                flag = jnp.full((BLOCK_TOKENS, 128), 1.0, jnp.bfloat16)
                if masked:
                    live = jnp.where(j < count, 1.0, 0.0).astype(jnp.float32)
                    value = (value.astype(jnp.float32) * live).astype(jnp.bfloat16)
                    flag = (jnp.full((BLOCK_TOKENS, 128), 1.0, jnp.float32) * live).astype(jnp.bfloat16)
                vs.append(jnp.concatenate([value, flag], axis=1))
            kc = jnp.concatenate(ks, axis=0)
            vc = jnp.concatenate(vs, axis=0)
            for r in range(rows // TILE):
                rs = pl.ds(r * TILE, TILE)
                s = lax.dot_general(
                    q_rows[rs, :], kc, (((1,), (1,)), ((), ())), preferred_element_type=jnp.float32
                )
                old = top_ref[rs, :]
                new = jnp.maximum(old, jnp.max(s, axis=1, keepdims=True))
                alpha = jnp.exp2((old - new) * EXP2_SCALE)
                wide = jnp.concatenate([new] * size, axis=1)
                p = jnp.exp2((s - wide) * EXP2_SCALE).astype(jnp.bfloat16)
                pv = jnp.dot(p, vc, preferred_element_type=jnp.float32)
                acc_ref[rs, :] = acc_ref[rs, :] * jnp.concatenate([alpha, alpha], axis=1) + pv
                top_ref[rs, :] = new

        full = count // BIG

        def big(c, carry):
            blocks(c * BIG, BIG, False)
            return carry

        def small(c, carry):
            blocks(full * BIG + c * SMALL, SMALL, True)
            return carry

        lax.fori_loop(0, full, big, 0)
        lax.fori_loop(0, (count - full * BIG + SMALL - 1) // SMALL, small, 0)
        tops, totals = [], []
        for h in range(heads):
            hc = slice(h * 128, (h + 1) * 128)
            out_ref[tokens, hc] = acc_ref[hc, :128].astype(jnp.bfloat16)
            tops.append(top_ref[hc, :])
            totals.append(acc_ref[hc, 128:])
        out_ref[tokens, heads * 128 :] = pack_stats(tops, totals, heads)
        return carry

    lax.fori_loop(0, query_blocks, query_block, 0)


def attention(ids, q, k, v):
    heads = q.shape[1] // HEAD_SIZE
    rows = heads * BLOCK_TOKENS
    vmem = pl.BlockSpec(memory_space=pltpu.VMEM)
    k = pltpu.with_memory_space_constraint(k, pltpu.VMEM)
    v = pltpu.with_memory_space_constraint(v, pltpu.VMEM)
    return pl.pallas_call(
        functools.partial(attention_kernel, heads),
        out_shape=jax.ShapeDtypeStruct((q.shape[0], q.shape[1] + 128), jnp.bfloat16),
        in_specs=[pl.BlockSpec(memory_space=pltpu.SMEM), vmem, vmem, vmem],
        out_specs=vmem,
        scratch_shapes=[
            pltpu.VMEM((rows, 128), jnp.bfloat16),
            pltpu.VMEM((rows, 128), jnp.float32),
            pltpu.VMEM((rows, 256), jnp.float32),
        ],
        compiler_params=pltpu.CompilerParams(vmem_limit_bytes=24 * 2**20),
        name="attend",
    )(ids, q, k, v)


def merge_kernel(heads, final, parts_ref, out_ref):
    sources, rows = parts_ref.shape[0], parts_ref.shape[1]
    wide = heads * 128
    step = 8
    for r in range(0, rows, step):
        rs = slice(r, r + step)

        def gather3(stats, first):
            total = stats if first == 0 else pltpu.roll(stats, 128 - first * heads, 1)
            for i in (1, 2):
                total = total + pltpu.roll(stats, 128 - (first + i) * heads, 1)
            return total

        stats = [parts_ref[s, rs, wide:].astype(jnp.float32) for s in range(sources)]
        tops = [gather3(x, 0) for x in stats]
        top = functools.reduce(jnp.maximum, tops)
        scales = [jnp.exp2((t - top) * EXP2_SCALE) for t in tops]
        total = functools.reduce(
            jnp.add, [gather3(x, 3) * scale for x, scale in zip(stats, scales)]
        )
        for h in range(heads):
            hc = slice(h * 128, (h + 1) * 128)
            acc = jnp.zeros((step, 128), jnp.float32)
            for s in range(sources):
                acc = acc + scales[s][:, h : h + 1] * parts_ref[s, rs, hc].astype(jnp.float32)
            if final:
                acc = acc / total[:, h : h + 1]
            out_ref[rs, hc] = acc.astype(jnp.bfloat16)
        if not final:
            spread = lambda x: [
                jnp.broadcast_to(x[:, h : h + 1], (step, 128)) for h in range(heads)
            ]
            out_ref[rs, wide:] = pack_stats(spread(top), spread(total), heads)


def merge(parts, final):
    width = parts.shape[2]
    heads = width // 128 - 1
    vmem = pl.BlockSpec(memory_space=pltpu.VMEM)
    return pl.pallas_call(
        functools.partial(merge_kernel, heads, final),
        out_shape=jax.ShapeDtypeStruct(
            (parts.shape[1], width - 128 if final else width), jnp.bfloat16
        ),
        in_specs=[vmem],
        out_specs=vmem,
        compiler_params=pltpu.CompilerParams(vmem_limit_bytes=12 * 2**20),
        name="merge",
    )(parts)


def project_kernel(place_ref, attended_ref, *refs):
    w_refs, out_ref = refs[:-1], refs[-1]
    count = len(w_refs)
    groups, _, rows, _ = out_ref.shape
    attended = attended_ref[...]
    for k, w_ref in enumerate(w_refs):
        place = lax.rem(place_ref[0] + (count - k), count)
        out = jnp.dot(attended, w_ref[...], preferred_element_type=jnp.float32)
        out = out.astype(jnp.bfloat16)
        for g in range(groups):
            out_ref[g, place] = out[g * rows : (g + 1) * rows]


def project(attended, weights, groups, axis):
    count = len(weights)
    vmem = pl.BlockSpec(memory_space=pltpu.VMEM)
    place = jnp.reshape(lax.axis_index(axis), (1,)).astype(jnp.int32)
    rows, cols = attended.shape[0] // groups, weights[0].shape[1]
    return pl.pallas_call(
        project_kernel,
        out_shape=jax.ShapeDtypeStruct((groups, count, rows, cols), jnp.bfloat16),
        in_specs=[pl.BlockSpec(memory_space=pltpu.SMEM)] + [vmem] * (1 + count),
        out_specs=vmem,
        compiler_params=pltpu.CompilerParams(vmem_limit_bytes=12 * 2**20),
        name="project",
    )(place, attended, *weights)


def swap(x, axis):
    return lax.all_to_all(x, axis, 0, 0, tiled=True)


def gather(x, axis):
    size = lax.axis_size(axis)
    out = swap(jnp.broadcast_to(x[None], (size, *x.shape)), axis)
    return out.reshape(size * x.shape[0], *x.shape[1:])


def scatter_sum(x, axis):
    size = lax.axis_size(axis)
    parts = swap(x.reshape(size, x.shape[0] // size, *x.shape[1:]), axis)
    return functools.reduce(jnp.add, [parts[i].astype(jnp.float32) for i in range(size)])


def on_device(text_states, w_query, w_out, visual_keys, visual_values, block_list):
    vis, hs = ("z", "y"), ("head", "sec")
    shards, ny, groups = (lax.axis_size(a) for a in (vis, "y", hs))
    weights = [w_out] + [
        lax.ppermute(w_out, "y", [(i, (i + k) % ny) for i in range(ny)]) for k in range(1, ny)
    ]
    terms = jnp.dot(text_states, w_query, preferred_element_type=jnp.float32)
    terms = scatter_sum(terms.astype(jnp.bfloat16), ("y", "z"))
    query = gather(gather(terms.astype(jnp.bfloat16), "z"), "y")
    ids = block_list[:, 0, :]
    partial = attention(ids, query, visual_keys, visual_values)
    attended = merge(swap(partial.reshape(shards, -1, partial.shape[1]), vis), True)
    out = project(gather(attended, "z"), weights, groups, "y")
    parts = swap(out.reshape(groups * ny, *out.shape[2:]), (*hs, "y")).reshape(out.shape)
    out = functools.reduce(jnp.add, [parts[g].astype(jnp.float32) for g in range(groups)])
    return out.astype(jnp.bfloat16).reshape(-1, out.shape[-1])


def solution(mesh):
    heads, vis, sec = (mesh.shape[a] for a in ("head", "vis", "sec"))
    ny = 4 if vis % 4 == 0 and vis > 4 else 2
    fine = Mesh(mesh.devices.reshape(heads, ny, vis // ny, sec), ("head", "y", "z", "sec"))
    vy, hs = ("y", "z"), ("head", "sec")
    in_specs = (
        P(None, vy),
        P(vy, hs),
        P(hs, vy),
        P(vy, hs),
        P(vy, hs),
        P(None, vy, None),
    )
    return jax.shard_map(
        on_device, mesh=fine, in_specs=in_specs, out_specs=P(hs, vy), check_vma=False
    )
```

```python
import functools

import jax
import jax.numpy as jnp
import numpy as np
from jax import lax
from jax.experimental import pallas as pl
from jax.experimental.pallas import tpu as pltpu
from jax.sharding import Mesh, PartitionSpec as P

HEAD_SIZE = 128
BLOCK_TOKENS = 128
BIG, MID, SMALL = 8, 4, 2
NEG_FILL = -1e30
EXP2_SCALE = float(np.log2(np.e) / np.sqrt(HEAD_SIZE))


def split3(x):
    hi = x.astype(jnp.bfloat16).astype(jnp.float32)
    rest = x - hi
    mid = rest.astype(jnp.bfloat16).astype(jnp.float32)
    return hi, mid, rest - mid


def pack_stats(top, total, heads):
    lane = lax.broadcasted_iota(jnp.int32, top[0].shape, 1)
    both = jnp.zeros(top[0].shape, jnp.float32)
    for h in range(heads):
        both = jnp.where(lane == h, top[h], both)
        both = jnp.where(lane == 3 * heads + h, total[h], both)
    hi, mid, low = split3(both)
    packed = hi + pltpu.roll(mid, heads, 1) + pltpu.roll(low, 2 * heads, 1)
    return packed.astype(jnp.bfloat16)


def attend_block(ids_ref, b, q_rows, k_ref, v_ref, top_ref, acc_ref):
    rows, slots = q_rows.shape[0], ids_ref.shape[1]
    tile = min(128, rows)
    top_ref[...] = jnp.full(top_ref.shape, NEG_FILL, jnp.float32)
    acc_ref[...] = jnp.zeros(acc_ref.shape, jnp.float32)
    count = lax.fori_loop(
        0, slots, lambda j, c: c + (ids_ref[b, j] >= 0).astype(jnp.int32), jnp.int32(0)
    )

    def blocks(first, size, masked):
        ks, vs = [], []
        for i in range(size):
            j = first + i
            block = ids_ref[b, jnp.minimum(j, count - 1) if masked else j]
            start = pl.multiple_of(block * BLOCK_TOKENS, BLOCK_TOKENS)
            ks.append(k_ref[pl.ds(start, BLOCK_TOKENS), :])
            value = v_ref[pl.ds(start, BLOCK_TOKENS), :]
            flag = jnp.full((BLOCK_TOKENS, 128), 1.0, jnp.bfloat16)
            if masked:
                live = jnp.where(j < count, 1.0, 0.0).astype(jnp.float32)
                value = (value.astype(jnp.float32) * live).astype(jnp.bfloat16)
                flag = (jnp.full((BLOCK_TOKENS, 128), 1.0, jnp.float32) * live).astype(jnp.bfloat16)
            vs.append(jnp.concatenate([value, flag], axis=1))
        kc = jnp.concatenate(ks, axis=0)
        vc = jnp.concatenate(vs, axis=0)
        for r in range(rows // tile):
            rs = pl.ds(r * tile, tile)
            s = lax.dot_general(
                q_rows[rs, :], kc, (((1,), (1,)), ((), ())), preferred_element_type=jnp.float32
            )
            old = top_ref[rs, :]
            new = jnp.maximum(old, jnp.max(s, axis=1, keepdims=True))
            alpha = jnp.exp2((old - new) * EXP2_SCALE)
            wide = jnp.concatenate([new] * size, axis=1)
            p = jnp.exp2((s - wide) * EXP2_SCALE).astype(jnp.bfloat16)
            pv = jnp.dot(p, vc, preferred_element_type=jnp.float32)
            acc_ref[rs, :] = acc_ref[rs, :] * jnp.concatenate([alpha, alpha], axis=1) + pv
            top_ref[rs, :] = new

    def big(c, carry):
        blocks(c * BIG, BIG, False)
        return carry

    def mid(c, carry):
        blocks(full * BIG, MID, False)
        return carry

    def small(c, carry):
        blocks(full * BIG + some * MID + c * SMALL, SMALL, True)
        return carry

    full = lax.shift_right_logical(count, 3)
    left = count - full * BIG
    some = lax.shift_right_logical(left, 2)
    rest = left - some * MID
    lax.fori_loop(0, full, big, 0)
    lax.fori_loop(0, some, mid, 0)
    lax.fori_loop(0, lax.shift_right_logical(rest + 1, 1), small, 0)


def near_kernel(heads, ids_ref, q_ref, k_ref, v_ref, out_ref, q_rows, top_ref, acc_ref):
    query_blocks, tokens = q_ref.shape[0], q_ref.shape[1]

    def query_block(b, carry):
        for h in range(heads):
            q_rows[h * tokens : (h + 1) * tokens, :] = q_ref[b, :, h * 128 : (h + 1) * 128]
        attend_block(ids_ref, b, q_rows, k_ref, v_ref, top_ref, acc_ref)
        tops, totals = [], []
        for h in range(heads):
            hr = slice(h * tokens, (h + 1) * tokens)
            out_ref[b, :, h * 128 : (h + 1) * 128] = acc_ref[hr, :128].astype(jnp.bfloat16)
            tops.append(top_ref[hr, :])
            totals.append(acc_ref[hr, 128:])
        out_ref[b, :, heads * 128 :] = pack_stats(tops, totals, heads)
        return carry

    lax.fori_loop(0, query_blocks, query_block, 0)


def far_kernel(
    heads, ids_ref, place_ref, near_ref, q_ref, k_ref, v_ref, out_ref, q_rows, top_ref, acc_ref
):
    count, query_blocks, tokens = q_ref.shape[:3]
    groups, rows = out_ref.shape[1], out_ref.shape[3]
    me = place_ref[0]

    def query_block(b, carry):
        for g in range(groups):
            out_ref[b, g, me] = near_ref[b, g * rows : (g + 1) * rows, :]
        for k in range(1, count):
            there = lax.rem(me + k, count)
            for h in range(heads):
                start = (h * (count - 1) + k - 1) * tokens
                q_rows[start : start + tokens, :] = q_ref[there, b, :, h * 128 : (h + 1) * 128]
        attend_block(ids_ref, b, q_rows, k_ref, v_ref, top_ref, acc_ref)
        for k in range(1, count):
            there = lax.rem(me + k, count)
            tops, totals = [], []
            for h in range(heads):
                start = (h * (count - 1) + k - 1) * tokens
                hr = slice(start, start + tokens)
                hc = slice(h * 128, (h + 1) * 128)
                acc = acc_ref[hr, :128].astype(jnp.bfloat16)
                for g in range(groups):
                    out_ref[b, g, there, :, hc] = acc[g * rows : (g + 1) * rows]
                tops.append(top_ref[hr, :])
                totals.append(acc_ref[hr, 128:])
            stats = pack_stats(tops, totals, heads)
            for g in range(groups):
                out_ref[b, g, there, :, heads * 128 :] = stats[g * rows : (g + 1) * rows]
        return carry

    lax.fori_loop(0, query_blocks, query_block, 0)


def scratch(rows):
    return [
        pltpu.VMEM((rows, 128), jnp.bfloat16),
        pltpu.VMEM((rows, 128), jnp.float32),
        pltpu.VMEM((rows, 256), jnp.float32),
    ]


def attend_near(ids, q, k, v):
    query_blocks, tokens, wide = q.shape
    heads = wide // HEAD_SIZE
    vmem, smem = (pl.BlockSpec(memory_space=m) for m in (pltpu.VMEM, pltpu.SMEM))
    return pl.pallas_call(
        functools.partial(near_kernel, heads),
        out_shape=jax.ShapeDtypeStruct((query_blocks, tokens, wide + 128), jnp.bfloat16),
        in_specs=[smem, vmem, vmem, vmem],
        out_specs=vmem,
        scratch_shapes=scratch(heads * tokens),
        compiler_params=pltpu.CompilerParams(vmem_limit_bytes=10 * 2**20),
        cost_estimate=pl.CostEstimate(flops=10**9, bytes_accessed=10**7, transcendentals=0),
        name="near",
    )(ids, q, k, v)


def attend_far(ids, place, near, q, k, v, groups):
    count, query_blocks, tokens, wide = q.shape
    heads = wide // HEAD_SIZE
    vmem, smem = (pl.BlockSpec(memory_space=m) for m in (pltpu.VMEM, pltpu.SMEM))
    return pl.pallas_call(
        functools.partial(far_kernel, heads),
        out_shape=jax.ShapeDtypeStruct(
            (query_blocks, groups, count, tokens // groups, wide + 128), jnp.bfloat16
        ),
        in_specs=[smem, smem, vmem, vmem, vmem, vmem],
        out_specs=vmem,
        scratch_shapes=scratch(heads * tokens * (count - 1)),
        compiler_params=pltpu.CompilerParams(vmem_limit_bytes=14 * 2**20),
        cost_estimate=pl.CostEstimate(flops=3 * 10**9, bytes_accessed=10**7, transcendentals=0),
        name="far",
    )(ids, place, near, q, k, v)


def terms_kernel(x_ref, w_ref, out_ref):
    out = jnp.dot(x_ref[...], w_ref[...], preferred_element_type=jnp.float32)
    out_ref[...] = out.astype(jnp.bfloat16)


def query_terms(x, w):
    rows, cols, step = x.shape[0], w.shape[1], 256
    return pl.pallas_call(
        terms_kernel,
        grid=(cols // step,),
        out_shape=jax.ShapeDtypeStruct((rows, cols), jnp.bfloat16),
        in_specs=[
            pl.BlockSpec(x.shape, lambda j: (0, 0)),
            pl.BlockSpec((w.shape[0], step), lambda j: (0, j)),
        ],
        out_specs=pl.BlockSpec((rows, step), lambda j: (0, j)),
        compiler_params=pltpu.CompilerParams(vmem_limit_bytes=12 * 2**20),
        name="terms",
    )(*(pltpu.with_memory_space_constraint(a, pltpu.HBM) for a in (x, w)))


def merge_kernel(heads, final, parts_ref, out_ref):
    sources, rows = parts_ref.shape[0], parts_ref.shape[1]
    wide = heads * 128
    step = 8
    for r in range(0, rows, step):
        rs = slice(r, r + step)

        def gather3(stats, first):
            total = stats if first == 0 else pltpu.roll(stats, 128 - first * heads, 1)
            for i in (1, 2):
                total = total + pltpu.roll(stats, 128 - (first + i) * heads, 1)
            return total

        stats = [parts_ref[s, rs, wide:].astype(jnp.float32) for s in range(sources)]
        tops = [gather3(x, 0) for x in stats]
        top = functools.reduce(jnp.maximum, tops)
        scales = [jnp.exp2((t - top) * EXP2_SCALE) for t in tops]
        total = functools.reduce(
            jnp.add, [gather3(x, 3) * scale for x, scale in zip(stats, scales)]
        )
        for h in range(heads):
            hc = slice(h * 128, (h + 1) * 128)
            acc = jnp.zeros((step, 128), jnp.float32)
            for s in range(sources):
                acc = acc + scales[s][:, h : h + 1] * parts_ref[s, rs, hc].astype(jnp.float32)
            if final:
                acc = acc / total[:, h : h + 1]
            out_ref[rs, hc] = acc.astype(jnp.bfloat16)
        if not final:
            spread = lambda x: [
                jnp.broadcast_to(x[:, h : h + 1], (step, 128)) for h in range(heads)
            ]
            out_ref[rs, wide:] = pack_stats(spread(top), spread(total), heads)


def merge(parts, final):
    width = parts.shape[2]
    heads = width // 128 - 1
    vmem = pl.BlockSpec(memory_space=pltpu.VMEM)
    return pl.pallas_call(
        functools.partial(merge_kernel, heads, final),
        out_shape=jax.ShapeDtypeStruct(
            (parts.shape[1], width - 128 if final else width), jnp.bfloat16
        ),
        in_specs=[vmem],
        out_specs=vmem,
        compiler_params=pltpu.CompilerParams(vmem_limit_bytes=12 * 2**20),
        name="merge",
    )(parts)


def project_kernel(place_ref, attended_ref, *refs):
    w_refs, out_ref = refs[:-1], refs[-1]
    count = len(w_refs)
    groups, _, rows, _ = out_ref.shape
    attended = attended_ref[...]
    for k, w_ref in enumerate(w_refs):
        place = lax.rem(place_ref[0] + (count - k), count)
        out = jnp.dot(attended, w_ref[...], preferred_element_type=jnp.float32)
        out = out.astype(jnp.bfloat16)
        for g in range(groups):
            out_ref[g, place] = out[g * rows : (g + 1) * rows]


def project(attended, weights, place, groups):
    count = len(weights)
    vmem = pl.BlockSpec(memory_space=pltpu.VMEM)
    rows, cols = attended.shape[0] // groups, weights[0].shape[1]
    return pl.pallas_call(
        project_kernel,
        out_shape=jax.ShapeDtypeStruct((groups, count, rows, cols), jnp.bfloat16),
        in_specs=[pl.BlockSpec(memory_space=pltpu.SMEM)] + [vmem] * (1 + count),
        out_specs=vmem,
        compiler_params=pltpu.CompilerParams(vmem_limit_bytes=12 * 2**20),
        name="project",
    )(place, attended, *weights)


def swap(x, axis):
    return lax.all_to_all(x, axis, 0, 0, tiled=True)


def gather(x, axis):
    size = lax.axis_size(axis)
    out = swap(jnp.broadcast_to(x[None], (size, *x.shape)), axis)
    return out.reshape(size * x.shape[0], *x.shape[1:])


def scatter_sum(x, axis):
    size = lax.axis_size(axis)
    parts = swap(x.reshape(size, x.shape[0] // size, *x.shape[1:]), axis)
    return functools.reduce(jnp.add, [parts[i].astype(jnp.float32) for i in range(size)])


def on_device(text_states, w_query, w_out, visual_keys, visual_values, block_list):
    vis, hs = ("z", "y"), ("head", "sec")
    ny, nz, groups = (lax.axis_size(a) for a in ("y", "z", hs))
    place = jnp.reshape(lax.axis_index("y"), (1,)).astype(jnp.int32)
    ids = block_list[:, 0, :]
    query_blocks = ids.shape[0]
    k = pltpu.with_memory_space_constraint(visual_keys, pltpu.VMEM)
    v = pltpu.with_memory_space_constraint(visual_values, pltpu.VMEM)
    terms = scatter_sum(query_terms(text_states, w_query), vis).astype(jnp.bfloat16)
    wide = terms.shape[1]
    mine = gather(terms, "z")
    near = attend_near(ids, mine.reshape(query_blocks, -1, wide), k, v)
    query = swap(jnp.broadcast_to(mine[None], (ny, *mine.shape)), "y")
    query, w_moved = lax.optimization_barrier((query, w_out))
    weights = [w_out] + [
        lax.ppermute(w_moved, "y", [(i, (i + d) % ny) for i in range(ny)]) for d in range(1, ny)
    ]
    query = query.reshape(ny, query_blocks, -1, wide)
    partial = attend_far(ids, place, near, query, k, v, nz // query_blocks)
    attended = merge(swap(partial.reshape(nz * ny, -1, wide + 128), vis), True)
    out = project(gather(attended, "z"), weights, place, groups)
    parts = swap(out.reshape(groups * ny, *out.shape[2:]), (*hs, "y")).reshape(out.shape)
    out = functools.reduce(jnp.add, [parts[g].astype(jnp.float32) for g in range(groups)])
    return out.astype(jnp.bfloat16).reshape(-1, out.shape[-1])


def solution(mesh):
    heads, vis, sec = (mesh.shape[a] for a in ("head", "vis", "sec"))
    ny = 4 if vis % 4 == 0 and vis > 4 else 2
    fine = Mesh(mesh.devices.reshape(heads, ny, vis // ny, sec), ("head", "y", "z", "sec"))
    vy, hs = ("y", "z"), ("head", "sec")
    in_specs = (
        P(None, vy),
        P(vy, hs),
        P(hs, vy),
        P(vy, hs),
        P(vy, hs),
        P(None, vy, None),
    )
    return jax.shard_map(
        on_device, mesh=fine, in_specs=in_specs, out_specs=P(hs, vy), check_vma=False
    )
```

```python
import functools

import jax
import jax.numpy as jnp
import numpy as np
from jax import lax
from jax.experimental import pallas as pl
from jax.experimental.pallas import tpu as pltpu
from jax.sharding import Mesh, PartitionSpec as P

HEAD_SIZE = 128
BLOCK_TOKENS = 128
BIG, MID, SMALL, TILE = 8, 4, 2, 128
NEG_FILL = -1e30
EXP2_SCALE = float(np.log2(np.e) / np.sqrt(HEAD_SIZE))


def split3(x):
    hi = x.astype(jnp.bfloat16).astype(jnp.float32)
    rest = x - hi
    mid = rest.astype(jnp.bfloat16).astype(jnp.float32)
    return hi, mid, rest - mid


def pack_stats(top, total, heads):
    lane = lax.broadcasted_iota(jnp.int32, top[0].shape, 1)
    both = jnp.zeros(top[0].shape, jnp.float32)
    for h in range(heads):
        both = jnp.where(lane == h, top[h], both)
        both = jnp.where(lane == 3 * heads + h, total[h], both)
    hi, mid, low = split3(both)
    packed = hi + pltpu.roll(mid, heads, 1) + pltpu.roll(low, 2 * heads, 1)
    return packed.astype(jnp.bfloat16)


def attention_kernel(heads, ids_ref, q_ref, k_ref, v_ref, out_ref, q_rows, top_ref, acc_ref):
    query_blocks = q_ref.shape[0] // BLOCK_TOKENS
    slots = ids_ref.shape[1]
    rows = heads * BLOCK_TOKENS

    def query_block(b, carry):
        tokens = pl.ds(pl.multiple_of(b * BLOCK_TOKENS, BLOCK_TOKENS), BLOCK_TOKENS)
        for h in range(heads):
            hc = slice(h * 128, (h + 1) * 128)
            q_rows[hc, :] = q_ref[tokens, hc]
        top_ref[...] = jnp.full(top_ref.shape, NEG_FILL, jnp.float32)
        acc_ref[...] = jnp.zeros(acc_ref.shape, jnp.float32)
        count = lax.fori_loop(
            0, slots, lambda j, c: c + (ids_ref[b, j] >= 0).astype(jnp.int32), jnp.int32(0)
        )

        def blocks(first, size, masked):
            ks, vs = [], []
            for i in range(size):
                j = first + i
                block = ids_ref[b, jnp.minimum(j, count - 1) if masked else j]
                start = pl.multiple_of(block * BLOCK_TOKENS, BLOCK_TOKENS)
                ks.append(k_ref[pl.ds(start, BLOCK_TOKENS), :])
                value = v_ref[pl.ds(start, BLOCK_TOKENS), :]
                flag = jnp.full((BLOCK_TOKENS, 128), 1.0, jnp.bfloat16)
                if masked:
                    live = jnp.where(j < count, 1.0, 0.0).astype(jnp.float32)
                    value = (value.astype(jnp.float32) * live).astype(jnp.bfloat16)
                    flag = (jnp.full((BLOCK_TOKENS, 128), 1.0, jnp.float32) * live).astype(jnp.bfloat16)
                vs.append(jnp.concatenate([value, flag], axis=1))
            kc = jnp.concatenate(ks, axis=0)
            vc = jnp.concatenate(vs, axis=0)
            for r in range(rows // TILE):
                rs = pl.ds(r * TILE, TILE)
                s = lax.dot_general(
                    q_rows[rs, :], kc, (((1,), (1,)), ((), ())), preferred_element_type=jnp.float32
                )
                old = top_ref[rs, :]
                new = jnp.maximum(old, jnp.max(s, axis=1, keepdims=True))
                alpha = jnp.exp2((old - new) * EXP2_SCALE)
                wide = jnp.concatenate([new] * size, axis=1)
                p = jnp.exp2((s - wide) * EXP2_SCALE).astype(jnp.bfloat16)
                pv = jnp.dot(p, vc, preferred_element_type=jnp.float32)
                acc_ref[rs, :] = acc_ref[rs, :] * jnp.concatenate([alpha, alpha], axis=1) + pv
                top_ref[rs, :] = new

        full = lax.shift_right_logical(count, 3)
        left = count - full * BIG
        some = lax.shift_right_logical(left, 2)
        rest = left - some * MID

        def big(c, carry):
            blocks(c * BIG, BIG, False)
            return carry

        def mid(c, carry):
            blocks(full * BIG, MID, False)
            return carry

        def small(c, carry):
            blocks(full * BIG + some * MID + c * SMALL, SMALL, True)
            return carry

        lax.fori_loop(0, full, big, 0)
        lax.fori_loop(0, some, mid, 0)
        lax.fori_loop(0, lax.shift_right_logical(rest + 1, 1), small, 0)
        tops, totals = [], []
        for h in range(heads):
            hc = slice(h * 128, (h + 1) * 128)
            out_ref[tokens, hc] = acc_ref[hc, :128].astype(jnp.bfloat16)
            tops.append(top_ref[hc, :])
            totals.append(acc_ref[hc, 128:])
        out_ref[tokens, heads * 128 :] = pack_stats(tops, totals, heads)
        return carry

    lax.fori_loop(0, query_blocks, query_block, 0)


def attention(ids, q, k, v):
    heads = q.shape[1] // HEAD_SIZE
    rows = heads * BLOCK_TOKENS
    vmem = pl.BlockSpec(memory_space=pltpu.VMEM)
    k = pltpu.with_memory_space_constraint(k, pltpu.VMEM)
    v = pltpu.with_memory_space_constraint(v, pltpu.VMEM)
    return pl.pallas_call(
        functools.partial(attention_kernel, heads),
        out_shape=jax.ShapeDtypeStruct((q.shape[0], q.shape[1] + 128), jnp.bfloat16),
        in_specs=[pl.BlockSpec(memory_space=pltpu.SMEM), vmem, vmem, vmem],
        out_specs=vmem,
        scratch_shapes=[
            pltpu.VMEM((rows, 128), jnp.bfloat16),
            pltpu.VMEM((rows, 128), jnp.float32),
            pltpu.VMEM((rows, 256), jnp.float32),
        ],
        compiler_params=pltpu.CompilerParams(vmem_limit_bytes=24 * 2**20),
        name="attend",
    )(ids, q, k, v)


def merge_kernel(heads, parts_ref, out_ref):
    sources, copies = parts_ref.shape[0], out_ref.shape[0]
    wide = heads * 128

    def gather3(stats, first):
        total = stats if first == 0 else pltpu.roll(stats, 128 - first * heads, 1)
        for i in (1, 2):
            total = total + pltpu.roll(stats, 128 - (first + i) * heads, 1)
        return total

    stats = [parts_ref[s, :, wide:].astype(jnp.float32) for s in range(sources)]
    tops = [gather3(x, 0) for x in stats]
    top = functools.reduce(jnp.maximum, tops)
    scales = [jnp.exp2((t - top) * EXP2_SCALE) for t in tops]
    total = functools.reduce(jnp.add, [gather3(x, 3) * scale for x, scale in zip(stats, scales)])
    for h in range(heads):
        hc = slice(h * 128, (h + 1) * 128)
        acc = jnp.zeros((parts_ref.shape[1], 128), jnp.float32)
        for s in range(sources):
            acc = acc + scales[s][:, h : h + 1] * parts_ref[s, :, hc].astype(jnp.float32)
        out = (acc / total[:, h : h + 1]).astype(jnp.bfloat16)
        for c in range(copies):
            out_ref[c, :, hc] = out


def merge(parts, copies):
    _, rows, width = parts.shape
    vmem = pl.BlockSpec(memory_space=pltpu.VMEM)
    return pl.pallas_call(
        functools.partial(merge_kernel, width // 128 - 1),
        out_shape=jax.ShapeDtypeStruct((copies, rows, width - 128), jnp.bfloat16),
        in_specs=[vmem],
        out_specs=vmem,
        compiler_params=pltpu.CompilerParams(vmem_limit_bytes=12 * 2**20),
        name="merge",
    )(parts)


def project_kernel(place_ref, attended_ref, *refs):
    w_refs, out_ref = refs[:-1], refs[-1]
    count = len(w_refs)
    groups, _, rows, _ = out_ref.shape
    attended = attended_ref[...]
    for k, w_ref in enumerate(w_refs):
        place = lax.rem(place_ref[0] + (count - k), count)
        out = jnp.dot(attended, w_ref[...], preferred_element_type=jnp.float32)
        out = out.astype(jnp.bfloat16)
        for g in range(groups):
            out_ref[g, place] = out[g * rows : (g + 1) * rows]


def project(attended, weights, groups, axis):
    count = len(weights)
    vmem = pl.BlockSpec(memory_space=pltpu.VMEM)
    place = jnp.reshape(lax.axis_index(axis), (1,)).astype(jnp.int32)
    rows, cols = attended.shape[0] // groups, weights[0].shape[1]
    return pl.pallas_call(
        project_kernel,
        out_shape=jax.ShapeDtypeStruct((groups, count, rows, cols), jnp.bfloat16),
        in_specs=[pl.BlockSpec(memory_space=pltpu.SMEM)] + [vmem] * (1 + count),
        out_specs=vmem,
        compiler_params=pltpu.CompilerParams(vmem_limit_bytes=12 * 2**20),
        name="project",
    )(place, attended, *weights)


def swap(x, axis):
    return lax.all_to_all(x, axis, 0, 0, tiled=True)


def total_of(parts):
    return functools.reduce(
        jnp.add, [parts[i].astype(jnp.float32) for i in range(parts.shape[0])]
    ).astype(jnp.bfloat16)


def copies(x, count):
    return jnp.broadcast_to(x[None], (count, *x.shape))


def on_device(text_states, w_query, w_out, visual_keys, visual_values, block_list):
    vis, hs = ("z", "y"), ("head", "sec")
    nz, ny, groups = (lax.axis_size(a) for a in ("z", "y", hs))
    weights = [w_out] + [
        lax.ppermute(w_out, "y", [(i, (i + k) % ny) for i in range(ny)]) for k in range(1, ny)
    ]
    terms = jnp.dot(text_states, w_query, preferred_element_type=jnp.float32).astype(jnp.bfloat16)
    terms = total_of(swap(terms.reshape(nz, -1, terms.shape[1]), "z"))
    terms = total_of(swap(copies(terms, ny), "y"))
    query = swap(copies(terms, nz), "z").reshape(-1, terms.shape[1])
    ids = block_list[:, 0, :]
    partial = attention(ids, query, visual_keys, visual_values)
    parts = swap(partial.reshape(nz * ny, -1, partial.shape[1]), vis)
    attended = swap(merge(parts, nz), "z")
    out = project(attended.reshape(-1, attended.shape[-1]), weights, groups, "y")
    parts = swap(out.reshape(groups * ny, *out.shape[2:]), (*hs, "y")).reshape(out.shape)
    return total_of(parts).reshape(-1, out.shape[-1])


def solution(mesh):
    heads, vis, sec = (mesh.shape[a] for a in ("head", "vis", "sec"))
    ny = 4 if vis % 4 == 0 and vis > 4 else 2
    fine = Mesh(mesh.devices.reshape(heads, ny, vis // ny, sec), ("head", "y", "z", "sec"))
    vy, hs = ("y", "z"), ("head", "sec")
    in_specs = (
        P(None, vy),
        P(vy, hs),
        P(hs, vy),
        P(vy, hs),
        P(vy, hs),
        P(None, vy, None),
    )
    return jax.shard_map(
        on_device, mesh=fine, in_specs=in_specs, out_specs=P(hs, vy), check_vma=False
    )
```

```python
import functools

import jax
import jax.numpy as jnp
import numpy as np
from jax import lax
from jax.experimental import pallas as pl
from jax.experimental.pallas import tpu as pltpu
from jax.sharding import Mesh, PartitionSpec as P

HEAD_SIZE = 128
BLOCK_TOKENS = 128
BIG, MID, SMALL, TILE = 8, 4, 2, 256
NEG_FILL = -1e30
EXP2_SCALE = float(np.log2(np.e) / np.sqrt(HEAD_SIZE))


def split3(x):
    hi = x.astype(jnp.bfloat16).astype(jnp.float32)
    rest = x - hi
    mid = rest.astype(jnp.bfloat16).astype(jnp.float32)
    return hi, mid, rest - mid


def pack_stats(top, total, heads):
    lane = lax.broadcasted_iota(jnp.int32, top[0].shape, 1)
    both = jnp.zeros(top[0].shape, jnp.float32)
    for h in range(heads):
        both = jnp.where(lane == h, top[h], both)
        both = jnp.where(lane == 3 * heads + h, total[h], both)
    hi, mid, low = split3(both)
    packed = hi + pltpu.roll(mid, heads, 1) + pltpu.roll(low, 2 * heads, 1)
    return packed.astype(jnp.bfloat16)


def attention_kernel(heads, ids_ref, q_ref, k_ref, v_ref, out_ref, q_rows, top_ref, acc_ref):
    query_blocks = q_ref.shape[0] // BLOCK_TOKENS
    slots = ids_ref.shape[1]
    rows = heads * BLOCK_TOKENS

    def query_block(b, carry):
        tokens = pl.ds(pl.multiple_of(b * BLOCK_TOKENS, BLOCK_TOKENS), BLOCK_TOKENS)
        for h in range(heads):
            hc = slice(h * 128, (h + 1) * 128)
            q_rows[hc, :] = q_ref[tokens, hc]
        top_ref[...] = jnp.full(top_ref.shape, NEG_FILL, jnp.float32)
        acc_ref[...] = jnp.zeros(acc_ref.shape, jnp.float32)
        count = lax.fori_loop(
            0, slots, lambda j, c: c + (ids_ref[b, j] >= 0).astype(jnp.int32), jnp.int32(0)
        )

        def blocks(first, size, masked):
            ks, vs = [], []
            for i in range(size):
                j = first + i
                block = ids_ref[b, jnp.minimum(j, count - 1) if masked else j]
                start = pl.multiple_of(block * BLOCK_TOKENS, BLOCK_TOKENS)
                ks.append(k_ref[pl.ds(start, BLOCK_TOKENS), :])
                value = v_ref[pl.ds(start, BLOCK_TOKENS), :]
                flag = jnp.full((BLOCK_TOKENS, 128), 1.0, jnp.bfloat16)
                if masked:
                    live = jnp.where(j < count, 1.0, 0.0).astype(jnp.float32)
                    value = (value.astype(jnp.float32) * live).astype(jnp.bfloat16)
                    flag = (jnp.full((BLOCK_TOKENS, 128), 1.0, jnp.float32) * live).astype(jnp.bfloat16)
                vs.append(jnp.concatenate([value, flag], axis=1))
            kc = jnp.concatenate(ks, axis=0)
            vc = jnp.concatenate(vs, axis=0)
            score = lambda r: lax.dot_general(
                q_rows[pl.ds(r * TILE, TILE), :],
                kc,
                (((1,), (1,)), ((), ())),
                preferred_element_type=jnp.float32,
            )
            tiles = rows // TILE
            ahead = score(0)
            for r in range(tiles):
                rs = pl.ds(r * TILE, TILE)
                s = ahead
                if r + 1 < tiles:
                    ahead = score(r + 1)
                old = top_ref[rs, :]
                new = jnp.maximum(old, jnp.max(s, axis=1, keepdims=True))
                alpha = jnp.exp2((old - new) * EXP2_SCALE)
                wide = jnp.concatenate([new] * size, axis=1)
                p = jnp.exp2((s - wide) * EXP2_SCALE).astype(jnp.bfloat16)
                pv = jnp.dot(p, vc, preferred_element_type=jnp.float32)
                acc_ref[rs, :] = acc_ref[rs, :] * jnp.concatenate([alpha, alpha], axis=1) + pv
                top_ref[rs, :] = new

        full = lax.shift_right_logical(count, 3)
        left = count - full * BIG
        some = lax.shift_right_logical(left, 2)
        rest = left - some * MID

        def big(c, carry):
            blocks(c * BIG, BIG, False)
            return carry

        def mid(c, carry):
            blocks(full * BIG, MID, False)
            return carry

        def small(c, carry):
            blocks(full * BIG + some * MID + c * SMALL, SMALL, True)
            return carry

        lax.fori_loop(0, full, big, 0)
        lax.fori_loop(0, some, mid, 0)
        lax.fori_loop(0, lax.shift_right_logical(rest + 1, 1), small, 0)
        tops, totals = [], []
        for h in range(heads):
            hc = slice(h * 128, (h + 1) * 128)
            out_ref[tokens, hc] = acc_ref[hc, :128].astype(jnp.bfloat16)
            tops.append(top_ref[hc, :])
            totals.append(acc_ref[hc, 128:])
        out_ref[tokens, heads * 128 :] = pack_stats(tops, totals, heads)
        return carry

    lax.fori_loop(0, query_blocks, query_block, 0)


def attention(ids, q, k, v):
    heads = q.shape[1] // HEAD_SIZE
    rows = heads * BLOCK_TOKENS
    vmem = pl.BlockSpec(memory_space=pltpu.VMEM)
    k = pltpu.with_memory_space_constraint(k, pltpu.VMEM)
    v = pltpu.with_memory_space_constraint(v, pltpu.VMEM)
    return pl.pallas_call(
        functools.partial(attention_kernel, heads),
        out_shape=jax.ShapeDtypeStruct((q.shape[0], q.shape[1] + 128), jnp.bfloat16),
        in_specs=[pl.BlockSpec(memory_space=pltpu.SMEM), vmem, vmem, vmem],
        out_specs=vmem,
        scratch_shapes=[
            pltpu.VMEM((rows, 128), jnp.bfloat16),
            pltpu.VMEM((rows, 128), jnp.float32),
            pltpu.VMEM((rows, 256), jnp.float32),
        ],
        compiler_params=pltpu.CompilerParams(vmem_limit_bytes=24 * 2**20),
        name="attend",
    )(ids, q, k, v)


def merge_kernel(heads, parts_ref, out_ref):
    sources, copies = parts_ref.shape[0], out_ref.shape[0]
    wide = heads * 128

    def gather3(stats, first):
        total = stats if first == 0 else pltpu.roll(stats, 128 - first * heads, 1)
        for i in (1, 2):
            total = total + pltpu.roll(stats, 128 - (first + i) * heads, 1)
        return total

    stats = [parts_ref[s, :, wide:].astype(jnp.float32) for s in range(sources)]
    tops = [gather3(x, 0) for x in stats]
    top = functools.reduce(jnp.maximum, tops)
    scales = [jnp.exp2((t - top) * EXP2_SCALE) for t in tops]
    total = functools.reduce(jnp.add, [gather3(x, 3) * scale for x, scale in zip(stats, scales)])
    for h in range(heads):
        hc = slice(h * 128, (h + 1) * 128)
        acc = jnp.zeros((parts_ref.shape[1], 128), jnp.float32)
        for s in range(sources):
            acc = acc + scales[s][:, h : h + 1] * parts_ref[s, :, hc].astype(jnp.float32)
        out = (acc / total[:, h : h + 1]).astype(jnp.bfloat16)
        for c in range(copies):
            out_ref[c, :, hc] = out


def merge(parts, copies):
    _, rows, width = parts.shape
    vmem = pl.BlockSpec(memory_space=pltpu.VMEM)
    return pl.pallas_call(
        functools.partial(merge_kernel, width // 128 - 1),
        out_shape=jax.ShapeDtypeStruct((copies, rows, width - 128), jnp.bfloat16),
        in_specs=[vmem],
        out_specs=vmem,
        compiler_params=pltpu.CompilerParams(vmem_limit_bytes=12 * 2**20),
        name="merge",
    )(parts)


def project_kernel(place_ref, attended_ref, *refs):
    w_refs, out_ref = refs[:-1], refs[-1]
    count = len(w_refs)
    groups, _, rows, _ = out_ref.shape
    attended = attended_ref[...]
    for k, w_ref in enumerate(w_refs):
        place = lax.rem(place_ref[0] + (count - k), count)
        out = jnp.dot(attended, w_ref[...], preferred_element_type=jnp.float32)
        out = out.astype(jnp.bfloat16)
        for g in range(groups):
            out_ref[g, place] = out[g * rows : (g + 1) * rows]


def project(attended, weights, groups, axis):
    count = len(weights)
    vmem = pl.BlockSpec(memory_space=pltpu.VMEM)
    place = jnp.reshape(lax.axis_index(axis), (1,)).astype(jnp.int32)
    rows, cols = attended.shape[0] // groups, weights[0].shape[1]
    return pl.pallas_call(
        project_kernel,
        out_shape=jax.ShapeDtypeStruct((groups, count, rows, cols), jnp.bfloat16),
        in_specs=[pl.BlockSpec(memory_space=pltpu.SMEM)] + [vmem] * (1 + count),
        out_specs=vmem,
        compiler_params=pltpu.CompilerParams(vmem_limit_bytes=12 * 2**20),
        name="project",
    )(place, attended, *weights)


def swap(x, axis):
    return lax.all_to_all(x, axis, 0, 0, tiled=True)


def total_of(parts):
    return functools.reduce(
        jnp.add, [parts[i].astype(jnp.float32) for i in range(parts.shape[0])]
    ).astype(jnp.bfloat16)


def copies(x, count):
    return jnp.broadcast_to(x[None], (count, *x.shape))


def on_device(text_states, w_query, w_out, visual_keys, visual_values, block_list):
    vis, hs = ("z", "y"), ("head", "sec")
    nz, ny, groups = (lax.axis_size(a) for a in ("z", "y", hs))
    weights = [w_out] + [
        lax.ppermute(w_out, "y", [(i, (i + d) % ny) for i in range(ny)])
        for d in range(1, ny)
    ]
    terms = jnp.dot(text_states, w_query, preferred_element_type=jnp.float32)
    terms = terms.astype(jnp.bfloat16)
    terms = total_of(swap(terms.reshape(nz * ny, -1, terms.shape[1]), ("y", "z")))
    query = swap(copies(terms, nz * ny), ("y", "z")).reshape(-1, terms.shape[1])
    ids = block_list[:, 0, :]
    partial = attention(ids, query, visual_keys, visual_values)
    parts = swap(partial.reshape(nz * ny, -1, partial.shape[1]), vis)
    attended = swap(merge(parts, nz), "z")
    out = project(attended.reshape(-1, attended.shape[-1]), weights, groups, "y")
    parts = swap(out.reshape(groups * ny, *out.shape[2:]), (*hs, "y")).reshape(out.shape)
    return total_of(parts).reshape(-1, out.shape[-1])


def solution(mesh):
    heads, vis, sec = (mesh.shape[a] for a in ("head", "vis", "sec"))
    ny = 4 if vis % 4 == 0 and vis > 4 else 2
    fine = Mesh(mesh.devices.reshape(heads, ny, vis // ny, sec), ("head", "y", "z", "sec"))
    vy, hs = ("y", "z"), ("head", "sec")
    in_specs = (
        P(None, vy),
        P(vy, hs),
        P(hs, vy),
        P(vy, hs),
        P(vy, hs),
        P(None, vy, None),
    )
    return jax.shard_map(
        on_device, mesh=fine, in_specs=in_specs, out_specs=P(hs, vy), check_vma=False
    )
```

```python
import functools

import jax
import jax.numpy as jnp
import numpy as np
from jax import lax
from jax.experimental import pallas as pl
from jax.experimental.pallas import tpu as pltpu
from jax.sharding import Mesh, PartitionSpec as P

HEAD_SIZE = 128
BLOCK_TOKENS = 128
BIG, MID, SMALL, TILE = 8, 4, 2, 256
NEG_FILL = -1e30
EXP2_SCALE = float(np.log2(np.e) / np.sqrt(HEAD_SIZE))


def split3(x):
    hi = x.astype(jnp.bfloat16).astype(jnp.float32)
    rest = x - hi
    mid = rest.astype(jnp.bfloat16).astype(jnp.float32)
    return hi, mid, rest - mid


def pack_stats(top, total, heads):
    lane = lax.broadcasted_iota(jnp.int32, top[0].shape, 1)
    both = jnp.zeros(top[0].shape, jnp.float32)
    for h in range(heads):
        both = jnp.where(lane == h, top[h], both)
        both = jnp.where(lane == 3 * heads + h, total[h], both)
    hi, mid, low = split3(both)
    packed = hi + pltpu.roll(mid, heads, 1) + pltpu.roll(low, 2 * heads, 1)
    return packed.astype(jnp.bfloat16)


def attention_kernel(heads, ids_ref, q_ref, k_ref, v_ref, out_ref, q_rows, top_ref, acc_ref):
    query_blocks = q_ref.shape[0] // BLOCK_TOKENS
    slots = ids_ref.shape[1]
    rows = heads * BLOCK_TOKENS

    def query_block(b, carry):
        tokens = pl.ds(pl.multiple_of(b * BLOCK_TOKENS, BLOCK_TOKENS), BLOCK_TOKENS)
        for h in range(heads):
            hc = slice(h * 128, (h + 1) * 128)
            q_rows[hc, :] = q_ref[tokens, hc]
        top_ref[...] = jnp.full(top_ref.shape, NEG_FILL, jnp.float32)
        acc_ref[...] = jnp.zeros(acc_ref.shape, jnp.float32)
        count = lax.fori_loop(
            0, slots, lambda j, c: c + (ids_ref[b, j] >= 0).astype(jnp.int32), jnp.int32(0)
        )

        def blocks(first, size, masked):
            ks, vs = [], []
            for i in range(size):
                j = first + i
                block = ids_ref[b, jnp.minimum(j, count - 1) if masked else j]
                start = pl.multiple_of(block * BLOCK_TOKENS, BLOCK_TOKENS)
                ks.append(k_ref[pl.ds(start, BLOCK_TOKENS), :])
                value = v_ref[pl.ds(start, BLOCK_TOKENS), :]
                flag = jnp.full((BLOCK_TOKENS, 128), 1.0, jnp.bfloat16)
                if masked:
                    live = jnp.where(j < count, 1.0, 0.0).astype(jnp.float32)
                    value = (value.astype(jnp.float32) * live).astype(jnp.bfloat16)
                    flag = (jnp.full((BLOCK_TOKENS, 128), 1.0, jnp.float32) * live).astype(jnp.bfloat16)
                vs.append(jnp.concatenate([value, flag], axis=1))
            kc = jnp.concatenate(ks, axis=0)
            vc = jnp.concatenate(vs, axis=0)
            score = lambda r: lax.dot_general(
                q_rows[pl.ds(r * TILE, TILE), :],
                kc,
                (((1,), (1,)), ((), ())),
                preferred_element_type=jnp.float32,
            )
            tiles = rows // TILE
            ahead = score(0)
            for r in range(tiles):
                rs = pl.ds(r * TILE, TILE)
                s = ahead
                if r + 1 < tiles:
                    ahead = score(r + 1)
                old = top_ref[rs, :]
                new = jnp.maximum(old, jnp.max(s, axis=1, keepdims=True))
                alpha = jnp.exp2((old - new) * EXP2_SCALE)
                wide = jnp.concatenate([new] * size, axis=1)
                p = jnp.exp2((s - wide) * EXP2_SCALE).astype(jnp.bfloat16)
                pv = jnp.dot(p, vc, preferred_element_type=jnp.float32)
                acc_ref[rs, :] = acc_ref[rs, :] * jnp.concatenate([alpha, alpha], axis=1) + pv
                top_ref[rs, :] = new

        full = lax.shift_right_logical(count, 3)
        left = count - full * BIG
        some = lax.shift_right_logical(left, 2)
        rest = left - some * MID

        def big(c, carry):
            blocks(c * BIG, BIG, False)
            return carry

        def mid(c, carry):
            blocks(full * BIG, MID, False)
            return carry

        def small(c, carry):
            blocks(full * BIG + some * MID + c * SMALL, SMALL, True)
            return carry

        lax.fori_loop(0, full, big, 0)
        lax.fori_loop(0, some, mid, 0)
        lax.fori_loop(0, lax.shift_right_logical(rest + 1, 1), small, 0)
        tops, totals = [], []
        for h in range(heads):
            hc = slice(h * 128, (h + 1) * 128)
            out_ref[tokens, hc] = acc_ref[hc, :128].astype(jnp.bfloat16)
            tops.append(top_ref[hc, :])
            totals.append(acc_ref[hc, 128:])
        out_ref[tokens, heads * 128 :] = pack_stats(tops, totals, heads)
        return carry

    lax.fori_loop(0, query_blocks, query_block, 0)


def attention(ids, q, k, v):
    heads = q.shape[1] // HEAD_SIZE
    rows = heads * BLOCK_TOKENS
    vmem = pl.BlockSpec(memory_space=pltpu.VMEM)
    k = pltpu.with_memory_space_constraint(k, pltpu.VMEM)
    v = pltpu.with_memory_space_constraint(v, pltpu.VMEM)
    return pl.pallas_call(
        functools.partial(attention_kernel, heads),
        out_shape=jax.ShapeDtypeStruct((q.shape[0], q.shape[1] + 128), jnp.bfloat16),
        in_specs=[pl.BlockSpec(memory_space=pltpu.SMEM), vmem, vmem, vmem],
        out_specs=vmem,
        scratch_shapes=[
            pltpu.VMEM((rows, 128), jnp.bfloat16),
            pltpu.VMEM((rows, 128), jnp.float32),
            pltpu.VMEM((rows, 256), jnp.float32),
        ],
        compiler_params=pltpu.CompilerParams(vmem_limit_bytes=24 * 2**20),
        name="attend",
    )(ids, q, k, v)


def merge_kernel(heads, parts_ref, out_ref):
    sources, copies = parts_ref.shape[0], out_ref.shape[0]
    wide = heads * 128

    def gather3(stats, first):
        total = stats if first == 0 else pltpu.roll(stats, 128 - first * heads, 1)
        for i in (1, 2):
            total = total + pltpu.roll(stats, 128 - (first + i) * heads, 1)
        return total

    stats = [parts_ref[s, :, wide:].astype(jnp.float32) for s in range(sources)]
    tops = [gather3(x, 0) for x in stats]
    top = functools.reduce(jnp.maximum, tops)
    scales = [jnp.exp2((t - top) * EXP2_SCALE) for t in tops]
    total = functools.reduce(jnp.add, [gather3(x, 3) * scale for x, scale in zip(stats, scales)])
    for h in range(heads):
        hc = slice(h * 128, (h + 1) * 128)
        acc = jnp.zeros((parts_ref.shape[1], 128), jnp.float32)
        for s in range(sources):
            acc = acc + scales[s][:, h : h + 1] * parts_ref[s, :, hc].astype(jnp.float32)
        out = (acc / total[:, h : h + 1]).astype(jnp.bfloat16)
        for c in range(copies):
            out_ref[c, :, hc] = out


def merge(parts, copies):
    _, rows, width = parts.shape
    vmem = pl.BlockSpec(memory_space=pltpu.VMEM)
    return pl.pallas_call(
        functools.partial(merge_kernel, width // 128 - 1),
        out_shape=jax.ShapeDtypeStruct((copies, rows, width - 128), jnp.bfloat16),
        in_specs=[vmem],
        out_specs=vmem,
        compiler_params=pltpu.CompilerParams(vmem_limit_bytes=12 * 2**20),
        name="merge",
    )(parts)


def project_kernel(place_ref, attended_ref, *refs):
    near, right, far_top, far_low, left, out_ref = refs
    half, count = far_top.shape[0], out_ref.shape[1]
    groups, _, rows, _ = out_ref.shape
    attended = attended_ref[...]
    whole = lambda w_ref: jnp.dot(attended, w_ref[...], preferred_element_type=jnp.float32)
    halves = jnp.dot(attended[:, :half], far_top[...], preferred_element_type=jnp.float32)
    halves = halves + jnp.dot(attended[:, half:], far_low[...], preferred_element_type=jnp.float32)
    for k, out in enumerate((whole(near), whole(right), halves, whole(left))):
        place = lax.rem(place_ref[0] + (count - k), count)
        out = out.astype(jnp.bfloat16)
        for g in range(groups):
            out_ref[g, place] = out[g * rows : (g + 1) * rows]


def project(attended, weights, groups, axis):
    count = lax.axis_size(axis)
    vmem = pl.BlockSpec(memory_space=pltpu.VMEM)
    place = jnp.reshape(lax.axis_index(axis), (1,)).astype(jnp.int32)
    rows, cols = attended.shape[0] // groups, weights[0].shape[1]
    return pl.pallas_call(
        project_kernel,
        out_shape=jax.ShapeDtypeStruct((groups, count, rows, cols), jnp.bfloat16),
        in_specs=[pl.BlockSpec(memory_space=pltpu.SMEM)] + [vmem] * (1 + len(weights)),
        out_specs=vmem,
        compiler_params=pltpu.CompilerParams(vmem_limit_bytes=12 * 2**20),
        name="project",
    )(place, attended, *weights)


def swap(x, axis):
    return lax.all_to_all(x, axis, 0, 0, tiled=True)


def total_of(parts):
    return functools.reduce(
        jnp.add, [parts[i].astype(jnp.float32) for i in range(parts.shape[0])]
    ).astype(jnp.bfloat16)


def copies(x, count):
    return jnp.broadcast_to(x[None], (count, *x.shape))


def on_device(text_states, w_query, w_out, visual_keys, visual_values, block_list):
    vis, hs = ("z", "y"), ("head", "sec")
    nz, ny, groups = (lax.axis_size(a) for a in ("z", "y", hs))
    shift = lambda x, d: lax.ppermute(x, "y", [(i, (i + d) % ny) for i in range(ny)])
    half = w_out.shape[0] // 2
    right, left = shift(w_out, 1), shift(w_out, 3)
    weights = [w_out, right, shift(w_out[:half], 2), shift(left[half:], 3), left]
    terms = jnp.dot(text_states, w_query, preferred_element_type=jnp.float32)
    terms = terms.astype(jnp.bfloat16)
    terms = total_of(swap(terms.reshape(nz * ny, -1, terms.shape[1]), ("y", "z")))
    mine = swap(copies(terms, nz), "z").reshape(-1, terms.shape[1])
    query = swap(copies(mine, ny), "y").reshape(-1, terms.shape[1])
    ids = block_list[:, 0, :]
    partial = attention(ids, query, visual_keys, visual_values)
    parts = swap(partial.reshape(nz * ny, -1, partial.shape[1]), vis)
    attended = swap(merge(parts, nz), "z")
    out = project(attended.reshape(-1, attended.shape[-1]), weights, groups, "y")
    parts = swap(out.reshape(groups * ny, *out.shape[2:]), (*hs, "y")).reshape(out.shape)
    return total_of(parts).reshape(-1, out.shape[-1])


def solution(mesh):
    heads, vis, sec = (mesh.shape[a] for a in ("head", "vis", "sec"))
    ny = 4 if vis % 4 == 0 and vis > 4 else 2
    fine = Mesh(mesh.devices.reshape(heads, ny, vis // ny, sec), ("head", "y", "z", "sec"))
    vy, hs = ("y", "z"), ("head", "sec")
    in_specs = (
        P(None, vy),
        P(vy, hs),
        P(hs, vy),
        P(vy, hs),
        P(vy, hs),
        P(None, vy, None),
    )
    return jax.shard_map(
        on_device, mesh=fine, in_specs=in_specs, out_specs=P(hs, vy), check_vma=False
    )
```
